32 devices in a mesh: ma: 4 (over y, x), freq: 8 (over z, core).
Axes of the slice: x: 2, y: 2, z: 4, core: 2. Of those that a mesh axis runs over, the one named last changes fastest.
Arguments:
- m_table: int32 [8], P('ma'), may hold values from 0 to 1023, as said below
- retained_modes: int32 [8], P('ma'), may hold values from 128 to 512, as said below
- cycle_ids: int32 [32], P('ma'), may hold values from 1 to 2047, as said below
- kl_coeffs: bfloat16 [8, 4, 512], P('ma', None, 'freq'), may hold values from -6 to 6
- kl_vectors: bfloat16 [8, 512, 32, 512], P('ma', 'freq'), may hold values from -0.375 to 0.375
- beam_matrix: bfloat16 [8, 32, 1024, 512], P('ma', 'freq'), may hold values from -0.00390625 to 0.00390625
Outputs:
- sky_maps: float32 [32, 2, 32, 2048], P('ma', None, 'freq')
The draws below stay inside these ranges and needn't reach their ends.
Inputs may be any that keep to these rules, and one draw needn't show every extreme that they name: `m_table`: all distinct; slots 2 q and 2 q + 1 hold two numbers that sum to 1023. `retained_modes`: some slot keeps all 512 modes. `cycle_ids`: all distinct.
All inputs are finite; a program needn't handle non-finite values.
Results may differ from the reference program's by a relative error of at most 0.01.
Values may be sent and summed in bfloat16 or wider, within the bound.
A program may use at most 64 MiB of HBM per device.

```python
import math
import jax
import jax.numpy as jnp
from jax import lax

MMAX = 1024
NPHI = 2048
L = 1024
K = 512
NKL = 512
CH = 32
NSIDE = 512
MM = 8
R = 32


def paired_slots(key):
    chosen = jax.random.permutation(jax.random.fold_in(key, 3), MMAX // 2)[:MM // 2]
    has_zero = jnp.any(chosen == 0)
    place = jax.random.randint(jax.random.fold_in(key, 4), (), 0, MM // 2)
    forced = jnp.where(jnp.arange(MM // 2) == place, 0, chosen)
    chosen = jnp.where(has_zero, chosen, forced)
    paired = jnp.stack([chosen, MMAX - 1 - chosen], axis=1)
    return paired.reshape(MM).astype(jnp.int32)


def draw_m_table(key, part):
    return paired_slots(key)


def draw_retained_modes(key, part):
    counts = jax.random.randint(jax.random.fold_in(key, 1), (MM,), NKL // 4, NKL + 1)
    fullest = jax.random.randint(jax.random.fold_in(key, 2), (), 0, MM)
    return jnp.where(jnp.arange(MM) == fullest, NKL, counts).astype(jnp.int32)


def draw_cycle_ids(key, part):
    return (jax.random.permutation(key, 4 * NSIDE - 1)[:R] + 1).astype(jnp.int32)


def draw_kl_coeffs(key, part):
    m_values = paired_slots(key).astype(jnp.float32)
    exponent = 2.0 * m_values / float(MMAX - 1) - 1.7
    slot_scale = jnp.exp(math.log(10.0) * exponent)
    value_key = jax.random.fold_in(key, 11)
    base = jnp.clip(jax.random.normal(value_key, (MM, 4, NKL), jnp.float32), -3.0, 3.0)
    values = jnp.clip(base * slot_scale[:, None, None], -6.0, 6.0)
    return values.astype(jnp.bfloat16)


def spiked(entries, own_key, source, target, shards_of, factor):
    owner, partner = [(jnp.arange(entries.shape[position]) // (entries.shape[position] // shards_of)).reshape([-1 if axis == position else 1 for axis in range(entries.ndim)]) for position in (source, target)]
    chosen = jax.random.permutation(own_key, shards_of)[partner]
    strong = (owner == chosen) | (owner == (partner + shards_of // 2) % shards_of)
    return jnp.where(strong, factor * entries, entries)


def shard_levels(own_key, shape, pieces, least, top_value):
    def one(position, shards_of):
        draws = jax.random.uniform(jax.random.fold_in(jax.random.fold_in(own_key, 6), position), (shards_of,), jnp.float32, least / len(pieces), top_value / len(pieces))
        return jnp.repeat(jnp.exp(draws), shape[position] // shards_of).reshape((-1,) + (1,) * (len(shape) - position - 1))

    level = one(*pieces[0])
    for cut in pieces[1:]:
        level = level * one(*cut)
    return level


def gaussian(key, shape, deviation, bound, pieces=(), held_as=jnp.bfloat16):
    array = jax.random.normal(key, shape, jnp.float32) * deviation
    if len(pieces) > 0:
        array = shard_levels(key, shape, pieces, -0.22, 0.18) * array
    return jnp.clip(array, min=-bound, max=bound).astype(held_as)


def heavy_noise(rng, dims, spread, bound, pieces, heavy, kind=jnp.bfloat16):
    result = spread * jax.random.normal(rng, dims, jnp.float32)
    if pieces:
        result = result * shard_levels(rng, dims, pieces, -0.22, 0.18)
    return jnp.clip(spiked(result, jax.random.fold_in(rng, 3), *heavy), -bound, bound).astype(kind)


def setup_inputs(seed: int = 0) -> dict:
    streams_of = jax.random.split(jax.random.key(seed), 7)
    return {
        "m_table": draw_m_table(jax.random.fold_in(streams_of[6], 71), 0),
        "retained_modes": draw_retained_modes(jax.random.fold_in(streams_of[6], 71), 0),
        "cycle_ids": draw_cycle_ids(jax.random.fold_in(streams_of[6], 71), 0),
        "kl_coeffs": draw_kl_coeffs(jax.random.fold_in(streams_of[6], 71), 0),
        "kl_vectors": heavy_noise(streams_of[4], (MM, NKL, CH, K), NKL ** -0.5, 0.375, ((0, 4), (1, 8)), (1, 2, 8, 2.0)),
        "beam_matrix": gaussian(streams_of[5], (MM, CH, L, K), (4 * K * L) ** -0.5, 0.00390625, ((0, 4), (1, 8))),
    }


def cycle_angles(cycle_numbers):
    cycle_float = cycle_numbers.astype(jnp.float32)
    nside_float = float(NSIDE)
    from_pole = jnp.minimum(cycle_float, 4.0 * nside_float - cycle_float)
    hemisphere = jnp.where(cycle_float <= 2.0 * nside_float, 1.0, -1.0)
    polar_part = from_pole * from_pole / (3.0 * nside_float * nside_float)
    colatitude_cosine = 1.0 - polar_part
    polar_sin = from_pole / (math.sqrt(3.0) * nside_float) * jnp.sqrt(2.0 - polar_part)
    latitude_cosine = 4.0 / 3.0 - 2.0 * from_pole / (3.0 * nside_float)
    latitude_sine = jnp.sqrt(jnp.maximum(1.0 - latitude_cosine * latitude_cosine, 0.25))
    in_cap = from_pole < nside_float
    cos_theta = hemisphere * jnp.where(in_cap, colatitude_cosine, latitude_cosine)
    sin_theta = jnp.where(in_cap, polar_sin, latitude_sine)
    return (cos_theta, sin_theta)

def combine(before_part, after_part):
    upper_left = after_part[0] * before_part[0] + after_part[1] * before_part[2]
    upper_right = after_part[0] * before_part[1] + after_part[1] * before_part[3]
    lower_left = after_part[2] * before_part[0] + after_part[3] * before_part[2]
    lower_right = after_part[2] * before_part[1] + after_part[3] * before_part[3]
    weight = jnp.abs(upper_left) + jnp.abs(upper_right) + jnp.abs(lower_left) + jnp.abs(lower_right)
    return (upper_left / weight, upper_right / weight, lower_left / weight, lower_right / weight, before_part[4] + after_part[4] + jnp.log(weight))

def legendre_rows(m_value, cos_theta, sin_theta):
    m_float = m_value.astype(jnp.float32)
    offset_rows = jnp.arange(L, dtype=jnp.float32)[:, None]
    later_rows = jnp.maximum(offset_rows, 2.0)
    degree = m_float + later_rows
    factor = jnp.sqrt((4.0 * degree * degree - 1.0) / (later_rows * (degree + m_float)))
    damping = jnp.sqrt((later_rows - 1.0) * (degree - 1.0 + m_float) / (4.0 * (degree - 1.0) * (degree - 1.0) - 1.0))
    first_step = jnp.sqrt(2.0 * m_float + 3.0)
    grid_shape = (L, cos_theta.shape[0])
    upper_left = jnp.where(offset_rows >= 2.0, factor * cos_theta[None, :], jnp.where(offset_rows >= 1.0, first_step * cos_theta[None, :], 1.0))
    upper_left = jnp.broadcast_to(upper_left, grid_shape)
    upper_right = jnp.broadcast_to(jnp.where(offset_rows >= 2.0, -factor * damping, 0.0), grid_shape)
    lower_left = jnp.broadcast_to(jnp.where(offset_rows >= 1.0, 1.0, 0.0), grid_shape)
    lower_right = jnp.broadcast_to(jnp.where(offset_rows >= 1.0, 0.0, 1.0), grid_shape)
    weight = jnp.abs(upper_left) + jnp.abs(upper_right) + jnp.abs(lower_left) + jnp.abs(lower_right)
    elements = (upper_left / weight, upper_right / weight, lower_left / weight, lower_right / weight, jnp.log(weight))
    prefix = lax.associative_scan(combine, elements, axis=0)
    log_start = 0.5 * (jnp.log((2.0 * m_float + 1.0) / (4.0 * math.pi)) + lax.lgamma(m_float + 0.5) - 0.5 * math.log(math.pi) - lax.lgamma(m_float + 1.0))
    log_start = log_start + m_float * jnp.log(sin_theta)[None, :]
    return prefix[0] * jnp.exp(prefix[4] + log_start)

def synthesize(harmonic_slot, m_value, cos_theta, sin_theta):
    channels = harmonic_slot.shape[0]
    flat_rows = harmonic_slot.reshape(channels * 4, L)
    padded = jnp.concatenate([flat_rows, jnp.zeros_like(flat_rows)], axis=1)
    shifted = lax.dynamic_slice_in_dim(padded, m_value.astype(jnp.int32), L, 1)
    legendre = legendre_rows(m_value, cos_theta, sin_theta).astype(jnp.bfloat16)
    synth_maps = jnp.dot(shifted, legendre, preferred_element_type=jnp.float32)
    return synth_maps.astype(jnp.bfloat16).reshape(channels, 2, 2, cos_theta.shape[0])

def fourier_table(m_values):
    azimuth_angle = jnp.arange(NPHI, dtype=jnp.int32)
    phase_index = m_values.astype(jnp.int32)[:, None] * azimuth_angle[None, :] % NPHI
    angle_table = phase_index.astype(jnp.float32) * (2.0 * math.pi / NPHI)
    weight = jnp.where(m_values == 0, 1.0, 2.0)[:, None]
    return jnp.stack([weight * jnp.cos(angle_table), -weight * jnp.sin(angle_table)]).astype(jnp.bfloat16)

def reference(m_table, retained_modes, cycle_ids, kl_coeffs, kl_vectors, beam_matrix):
    cos_theta, sin_theta = cycle_angles(cycle_ids)

    def per_slot(slot_entry):
        coeffs, vectors, beam_position, m_value, kept_count = slot_entry
        mode_index = jnp.arange(NKL, dtype=jnp.int32)
        masked = jnp.where(mode_index[None, :] < kept_count, coeffs, jnp.zeros_like(coeffs))
        svd_flat = jnp.dot(masked, vectors.reshape(NKL, CH * K), preferred_element_type=jnp.float32)
        singular_coefficients = svd_flat.astype(jnp.bfloat16).reshape(4, CH, K)
        spherical_harmonic = jnp.einsum('exd,xgd->xeg', singular_coefficients.astype(jnp.float32), beam_position.astype(jnp.float32)).astype(jnp.bfloat16)
        return synthesize(spherical_harmonic, m_value, cos_theta, sin_theta)
    cycle_modes = lax.map(per_slot, (kl_coeffs, kl_vectors, beam_matrix, m_table, retained_modes))
    fourier = fourier_table(m_table)
    return jnp.einsum('mcsqr,qmt->rsct', cycle_modes.astype(jnp.float32), fourier.astype(jnp.float32))
```

```python
import functools
import math

import jax
import jax.numpy as jnp
from jax import lax
from jax.experimental import pallas as pl
from jax.experimental.pallas import tpu as pltpu
from jax.sharding import PartitionSpec as P

NPHI = 2048
NSIDE = 512
SEGMENTS = 8
MESH = pl.DeviceIdType.MESH
F32 = jnp.float32
BF16 = jnp.bfloat16
BIG = 2.0**30
SHRINK = 2.0**-60


def cycle_angles(cycle_numbers):
    cycle_float = cycle_numbers.astype(F32)
    nside_float = float(NSIDE)
    from_pole = jnp.minimum(cycle_float, 4.0 * nside_float - cycle_float)
    hemisphere = jnp.where(cycle_float <= 2.0 * nside_float, 1.0, -1.0)
    polar_part = from_pole * from_pole / (3.0 * nside_float * nside_float)
    polar_sin = from_pole / (math.sqrt(3.0) * nside_float) * jnp.sqrt(2.0 - polar_part)
    latitude_cosine = 4.0 / 3.0 - 2.0 * from_pole / (3.0 * nside_float)
    latitude_sine = jnp.sqrt(jnp.maximum(1.0 - latitude_cosine * latitude_cosine, 0.25))
    in_cap = from_pole < nside_float
    cos_theta = hemisphere * jnp.where(in_cap, 1.0 - polar_part, latitude_cosine)
    sin_theta = jnp.where(in_cap, polar_sin, latitude_sine)
    return (cos_theta, sin_theta)


def fourier_table(m_values):
    azimuth_angle = jnp.arange(NPHI, dtype=jnp.int32)
    phase_index = m_values[:, None] * azimuth_angle[None, :] % NPHI
    angle_table = phase_index.astype(F32) * (2.0 * math.pi / NPHI)
    weight = jnp.where(m_values == 0, 1.0, 2.0)[:, None]
    return jnp.stack([weight * jnp.cos(angle_table), -weight * jnp.sin(angle_table)]).astype(BF16)


def central_ratio(m_float):
    shifted = m_float + 0.25
    inverse = 1.0 / (shifted * shifted)
    series = 1.0 + inverse * (-1.0 / 64.0 + inverse * (21.0 / 8192.0))
    ratio = series / jnp.sqrt(math.pi * shifted)
    exact = 1.0
    for m in range(8):
        ratio = jnp.where(m_float == float(m), exact, ratio)
        exact = exact * (2 * m + 1) / (2 * m + 2)
    return ratio


def gather_kernel(
    n_ma, n_freq, m_ref, kept_ref, cyc_ref, coef_ref, vec_hbm, ints_out, svd_out,
    ints, ints_send, vec, send, recv, vec_sem, isend_sem, irecv_sem, send_sem, recv_sem,
):
    slots, quads, modes = coef_ref.shape
    channels, depth = vec_hbm.shape[2], vec_hbm.shape[3]
    n_cyc = cyc_ref.shape[0]
    rows = quads * channels
    block_rows = rows // n_freq
    ma, fr = lax.axis_index("ma"), lax.axis_index("freq")
    pieces = [
        pltpu.make_async_copy(vec_hbm.at[s], vec.at[s], vec_sem.at[s]) for s in range(slots)
    ]
    for piece in pieces:
        piece.start()
    barrier = pltpu.get_barrier_semaphore()
    for k in range(1, n_ma):
        pl.semaphore_signal(
            barrier, inc=1, device_id=(lax.rem(ma + k, n_ma), fr), device_id_type=MESH
        )
    for k in range(1, n_freq):
        pl.semaphore_signal(
            barrier, inc=1, device_id=(ma, lax.rem(fr + k, n_freq)), device_id_type=MESH
        )
    lane = lax.broadcasted_iota(jnp.int32, (8, 128), 1)
    packed = jnp.zeros((8, 128), jnp.int32)
    for i in range(n_cyc):
        packed = jnp.where(lane == i, cyc_ref[i], packed)
    for s in range(slots):
        packed = jnp.where(lane == n_cyc + s, m_ref[s], packed)
    ints_send[...] = packed
    wide = modes * channels
    row = lax.broadcasted_iota(jnp.int32, (rows, wide), 0)
    column = lax.broadcasted_iota(jnp.int32, (rows, wide), 1)
    same_channel = row // quads == column % channels
    spread = (
        lax.broadcasted_iota(jnp.int32, (modes, wide), 1) // channels
        == lax.broadcasted_iota(jnp.int32, (modes, wide), 0)
    )
    spread = jnp.where(spread, 1.0, 0.0).astype(BF16)
    repeat = (
        lax.broadcasted_iota(jnp.int32, (rows, quads), 0) % quads
        == lax.broadcasted_iota(jnp.int32, (rows, quads), 1)
    )
    repeat = jnp.where(repeat, 1.0, 0.0).astype(BF16)
    mode = fr * modes + lax.broadcasted_iota(jnp.int32, (quads, modes), 1)
    pl.semaphore_wait(barrier, n_ma - 1 + n_freq - 1)
    int_copies = []
    for k in range(1, n_ma):
        copy = pltpu.make_async_remote_copy(
            src_ref=ints_send, dst_ref=ints.at[k], send_sem=isend_sem.at[k],
            recv_sem=irecv_sem.at[k], device_id=(lax.rem(ma + k, n_ma), fr), device_id_type=MESH,
        )
        copy.start()
        int_copies.append(copy)
    for s in range(slots):
        masked = jnp.where(mode < kept_ref[s], coef_ref[s].astype(F32), 0.0).astype(BF16)
        tall = jnp.dot(repeat, masked, preferred_element_type=F32).astype(BF16)
        full = jnp.dot(tall, spread, preferred_element_type=F32)
        weights = jnp.where(same_channel, full, 0.0).astype(BF16)
        pieces[s].wait()
        flat = vec[s].reshape(wide, depth)
        part = jnp.dot(weights, flat, preferred_element_type=F32).astype(BF16)
        for f in range(n_freq):
            send[f, s] = part[f * block_rows : (f + 1) * block_rows]
    copies = []
    for k in range(1, n_freq):
        to = lax.rem(fr + k, n_freq)
        copy = pltpu.make_async_remote_copy(
            src_ref=send.at[to], dst_ref=recv.at[k], send_sem=send_sem.at[k],
            recv_sem=recv_sem.at[k], device_id=(ma, to), device_id_type=MESH,
        )
        copy.start()
        copies.append(copy)
    for copy in int_copies:
        copy.wait()
    ints_out[0] = packed
    for k in range(1, n_ma):
        ints_out[k] = ints[k]
    total = send[fr].astype(F32)
    for k in range(1, n_freq):
        copies[k - 1].wait()
        total = total + recv[k].astype(F32)
    svd_out[...] = total.astype(BF16)


def gather_call(n_ma, n_freq, m_table, retained_modes, cycle_ids, kl_coeffs, kl_vectors):
    slots, quads, modes = kl_coeffs.shape
    channels, depth = kl_vectors.shape[2:]
    block_rows = quads * channels // n_freq
    smem = pl.BlockSpec(memory_space=pltpu.SMEM)
    vmem = pl.BlockSpec(memory_space=pltpu.VMEM)
    return pl.pallas_call(
        functools.partial(gather_kernel, n_ma, n_freq),
        out_shape=(
            jax.ShapeDtypeStruct((n_ma, 8, 128), jnp.int32),
            jax.ShapeDtypeStruct((slots, block_rows, depth), BF16),
        ),
        in_specs=[smem, smem, smem, vmem, pl.BlockSpec(memory_space=pl.ANY)],
        out_specs=(vmem, vmem),
        scratch_shapes=[
            pltpu.VMEM((n_ma, 8, 128), jnp.int32),
            pltpu.VMEM((8, 128), jnp.int32),
            pltpu.VMEM(kl_vectors.shape, BF16),
            pltpu.VMEM((n_freq, slots, block_rows, depth), BF16),
            pltpu.VMEM((n_freq, slots, block_rows, depth), BF16),
            pltpu.SemaphoreType.DMA((slots,)),
            pltpu.SemaphoreType.DMA((n_ma,)),
            pltpu.SemaphoreType.DMA((n_ma,)),
            pltpu.SemaphoreType.DMA((n_freq,)),
            pltpu.SemaphoreType.DMA((n_freq,)),
        ],
        compiler_params=pltpu.CompilerParams(collective_id=0, has_side_effects=True),
        name="gather_svd",
    )(m_table, retained_modes, cycle_ids, kl_coeffs, kl_vectors)


def legendre_into(par_ref, rows_ref, exps_ref, leg_ref):
    length, _, wide = rows_ref.shape
    half = wide // 2
    shape = (SEGMENTS, wide)
    m = jnp.broadcast_to(par_ref[0:1, :], shape)
    c = jnp.broadcast_to(par_ref[1:2, :], shape)
    first = lax.broadcasted_iota(jnp.int32, shape, 1) < half
    base = (lax.broadcasted_iota(jnp.int32, shape, 0) * length).astype(F32)

    def ratio(degree):
        after = degree - m > 0.5
        y = (degree - m) * (degree + m) / ((2.0 * degree - 1.0) * (2.0 * degree + 1.0))
        y = jnp.where(after, y, 1.0)
        a = lax.rsqrt(y)
        a = a * (1.5 - 0.5 * y * a * a)
        return (after, a, jnp.where(after, y * a, 0.0))

    steps = 4

    def body(i, state):
        p1, p2, e, root = state
        for u in range(steps):
            j = i * steps + u
            after, a, next_root = ratio(base + j.astype(F32))
            p = jnp.where(after, a * c, 1.0) * p1 - a * root * p2
            p1, p2, root = p, p1, next_root
            rows_ref[j] = p
            exps_ref[j] = e
        large = jnp.maximum(jnp.abs(p1), jnp.abs(p2)) > BIG
        scale = jnp.where(large, SHRINK, 1.0)
        return (p1 * scale, p2 * scale, jnp.where(large, e + 60.0, e), root)

    one = jnp.where(first, 1.0, 0.0)
    lax.fori_loop(
        0, length // steps, body,
        (one, 1.0 - one, jnp.zeros(shape, F32), ratio(base - 1.0)[2]), unroll=2,
    )
    last, last_e = rows_ref[length - 1], exps_ref[length - 1]
    before, before_e = rows_ref[length - 2], exps_ref[length - 2]
    top = jnp.maximum(last_e, pltpu.roll(last_e, half, 1))
    last = last * jnp.exp2(jnp.maximum(last_e - top, -126.0))
    before = before * jnp.exp2(jnp.maximum(before_e - top, -126.0))
    x = jnp.where(first[0:1], par_ref[2:3, :], 0.0)
    x_e = par_ref[3:4, :]
    starts, starts_e = [], []
    for s in range(SEGMENTS):
        starts.append(x)
        starts_e.append(x_e)
        if s < SEGMENTS - 1:
            t1, t2 = x * last[s : s + 1], x * before[s : s + 1]
            t1, t2 = t1 + pltpu.roll(t1, half, 1), t2 + pltpu.roll(t2, half, 1)
            size = jnp.maximum(jnp.abs(t1), jnp.abs(t2))
            x = jnp.where(first[0:1], t1, t2)
            large, small = size > BIG, size < 1.0 / BIG
            x = x * jnp.where(large, SHRINK, jnp.where(small, 1.0 / SHRINK, 1.0))
            x_e = x_e + top[s : s + 1] + jnp.where(large, 60.0, jnp.where(small, -60.0, 0.0))
    for s in range(SEGMENTS):
        exponent = exps_ref[:, s, :] + starts_e[s]
        low = jnp.floor(exponent * 0.5)
        degree = (
            s * length + lax.broadcasted_iota(jnp.int32, (length, wide), 0)
        ).astype(F32)
        value = rows_ref[:, s, :] * jnp.exp2(jnp.maximum(low, -126.0)) * starts[s]
        value = value * jnp.exp2(jnp.maximum(exponent - low, -126.0))
        value = jnp.where(degree >= par_ref[0:1, :], value, 0.0)
        turned = value.T
        leg_ref[:, s * length : (s + 1) * length] = (turned[:half] + turned[half:]).astype(BF16)


def synth_kernel(par_ref, svd_ref, beam_ref, out_ref, rows_ref, exps_ref, leg_ref):
    s, c = pl.program_id(0), pl.program_id(1)
    slots, block_rows, depth = svd_ref.shape
    n_ch = pl.num_programs(1)
    cycles = leg_ref.shape[0] // slots
    quads = 4

    @pl.when((s == 0) & (c == 0))
    def _():
        legendre_into(par_ref, rows_ref, exps_ref, leg_ref)
        out_ref[...] = jnp.zeros_like(out_ref)

    leg = leg_ref[pl.ds(pl.multiple_of(s * cycles, cycles), cycles), :]
    table = jnp.dot(leg, beam_ref[0, 0], preferred_element_type=F32).astype(BF16)
    svd = svd_ref[...].reshape(slots * block_rows, depth)
    svd = jnp.concatenate([svd, jnp.zeros((128 - slots * block_rows, depth), BF16)], axis=0)
    modes = lax.dot_general(
        table, svd, (((1,), (1,)), ((), ())), preferred_element_type=F32
    )
    group = lax.broadcasted_iota(jnp.int32, modes.shape, 1) // quads
    out_ref[...] += jnp.where(group == s * n_ch + c, modes, 0.0)


def synth_call(params, svd, beam_matrix, cycles):
    slots, channels, length, depth = beam_matrix.shape
    wide = params.shape[1]
    return pl.pallas_call(
        synth_kernel,
        grid=(slots, channels),
        out_shape=jax.ShapeDtypeStruct((cycles, 128), F32),
        in_specs=[
            pl.BlockSpec(params.shape, lambda s, c: (0, 0)),
            pl.BlockSpec(svd.shape, lambda s, c: (0, 0, 0)),
            pl.BlockSpec((1, 1, length, depth), lambda s, c: (s, c, 0, 0)),
        ],
        out_specs=pl.BlockSpec((cycles, 128), lambda s, c: (0, 0)),
        scratch_shapes=[
            pltpu.VMEM((length // SEGMENTS, SEGMENTS, wide), F32),
            pltpu.VMEM((length // SEGMENTS, SEGMENTS, wide), F32),
            pltpu.VMEM((slots * cycles, length), BF16),
        ],
        name="synth_cycles",
    )(params, svd, beam_matrix)


def swap_kernel(n_ma, in_ref, out_ref, recv, send_sem, recv_sem):
    ma, fr = lax.axis_index("ma"), lax.axis_index("freq")
    mine = recv.shape[1]
    barrier = pltpu.get_barrier_semaphore()
    for k in range(1, n_ma):
        pl.semaphore_signal(
            barrier, inc=1, device_id=(lax.rem(ma + k, n_ma), fr), device_id_type=MESH
        )
    pl.semaphore_wait(barrier, n_ma - 1)
    copies = []
    for k in range(1, n_ma):
        to = lax.rem(ma + k, n_ma)
        copy = pltpu.make_async_remote_copy(
            src_ref=in_ref.at[pl.ds(pl.multiple_of(to * mine, mine), mine)],
            dst_ref=recv.at[k], send_sem=send_sem.at[k], recv_sem=recv_sem.at[k],
            device_id=(to, fr), device_id_type=MESH,
        )
        copy.start()
        copies.append(copy)
    out_ref[0] = in_ref[pl.ds(pl.multiple_of(ma * mine, mine), mine)]
    for k in range(1, n_ma):
        copies[k - 1].wait()
        out_ref[k] = recv[k]


def swap_call(n_ma, modes):
    mine = modes.shape[0] // n_ma
    vmem = pl.BlockSpec(memory_space=pltpu.VMEM)
    return pl.pallas_call(
        functools.partial(swap_kernel, n_ma),
        out_shape=jax.ShapeDtypeStruct((n_ma, mine, 128), F32),
        in_specs=[vmem],
        out_specs=vmem,
        scratch_shapes=[
            pltpu.VMEM((n_ma, mine, 128), F32),
            pltpu.SemaphoreType.DMA((n_ma,)),
            pltpu.SemaphoreType.DMA((n_ma,)),
        ],
        compiler_params=pltpu.CompilerParams(collective_id=1, has_side_effects=True),
        name="swap_cycles",
    )(modes)


def local(n_ma, n_freq, m_table, retained_modes, cycle_ids, kl_coeffs, kl_vectors, beam_matrix):
    slots, n_cyc = m_table.shape[0], cycle_ids.shape[0]
    channels, length = beam_matrix.shape[1:3]
    cycles = n_cyc * n_ma
    ints, svd = gather_call(
        n_ma, n_freq, m_table, retained_modes, cycle_ids, kl_coeffs, kl_vectors
    )
    ma = lax.axis_index("ma")
    numbers = ints[:, 0, :]
    source = lax.rem(ma - jnp.arange(n_ma) + n_ma, n_ma)
    cos_theta, sin_theta = cycle_angles(
        numbers[:, :n_cyc].reshape(cycles)
    )
    m_float = m_table.astype(F32)[:, None]
    mantissa = jnp.sqrt((2.0 * m_float + 1.0) / (4.0 * math.pi) * central_ratio(m_float))
    power = m_float * (jnp.log(sin_theta) * (1.0 / math.log(2.0)))[None, :]
    whole = jnp.floor(power)
    mantissa = mantissa * jnp.exp2(power - whole)
    both = lambda a: jnp.tile(jnp.broadcast_to(a, (slots, cycles)).reshape(1, -1), (1, 2))
    params = jnp.concatenate(
        [both(m_float), both(cos_theta[None, :]), both(mantissa), both(whole)]
        + [jnp.zeros((4, 2 * slots * cycles), F32)], axis=0
    )
    modes = synth_call(params, svd, beam_matrix, cycles)
    modes = modes.reshape(n_ma, n_cyc, 128)[source].reshape(cycles, 128)
    swapped = swap_call(n_ma, modes)[:, :, : slots * channels * 4]
    swapped = swapped.reshape(n_ma, n_cyc, slots, channels, 2, 2).astype(BF16)
    fourier = fourier_table(numbers[:, n_cyc : n_cyc + slots].reshape(n_ma * slots))
    fourier = fourier.reshape(2, n_ma, slots, NPHI)
    return jnp.einsum("arscde,east->rdct", swapped, fourier, preferred_element_type=F32)


def solution(mesh):
    placed = (
        P("ma"),
        P("ma"),
        P("ma"),
        P("ma", None, "freq"),
        P("ma", "freq", None, None),
        P("ma", "freq", None, None),
    )
    return jax.shard_map(
        functools.partial(local, mesh.shape["ma"], mesh.shape["freq"]),
        mesh=mesh, in_specs=placed, out_specs=P("ma", None, "freq", None), check_vma=False,
    )
```
